32 devices in a mesh: lon: 8 (over z, y), lat: 4 (over x, core).
Axes of the slice: x: 2, y: 2, z: 4, core: 2. Of those that a mesh axis runs over, the one named last changes fastest.
Arguments:
- zonal_velocity: float32 [40, 64, 1024], P(None, 'lat', 'lon'), as said below
- northward_velocity: float32 [40, 64, 1024], P(None, 'lat', 'lon'), as said below
- level_count: int32 [64, 1024], P('lat', 'lon'), may hold values from 0 to 40, as said below
- surface_height: float32 [64, 1024], P('lat', 'lon'), may hold values from -4 to 4
- zonal_transport: float32 [64, 1024], P('lat', 'lon'), may hold values from -4 to 4
- northward_transport: float32 [64, 1024], P('lat', 'lon'), may hold values from -4 to 4
- thickness: float32 [40], replicated, may hold values from 0.015 to 0.06
Outputs:
- zonal_after: float32 [40, 64, 1024], P(None, 'lat', 'lon')
- northward_after: float32 [40, 64, 1024], P(None, 'lat', 'lon')
- surface_after: float32 [64, 1024], P('lat', 'lon')
- zonal_mean: float32 [64, 1024], P('lat', 'lon')
- northward_mean: float32 [64, 1024], P('lat', 'lon')
The draws below stay inside these ranges and needn't reach their ends.
Inputs may be any that keep to these rules, and one draw needn't show every extreme that they name: `level_count`: ocean cells have 4 to 40 levels and land cells 0; the first and the last latitude rows are land. `zonal_velocity`: zero at every level k (counted from 0) with k >= min(level_count of the cell, level_count of its eastern neighbour), longitude wrapping. `northward_velocity`: zero at every level k (counted from 0) with k >= min(level_count of the cell, level_count of its northern neighbour), latitude wrapping.
All inputs are finite; a program needn't handle non-finite values.
Results may differ from the reference program's by a relative error of at most 0.0003.
Values sent between devices are 32-bit elements; how exact they have to be, the bound alone decides.
A program may use at most 64 MiB of HBM per device.

```python
import math
import jax
import jax.numpy as jnp
from jax import lax

CLAT = 16
CLON = 128
NZ = 40
NSUB = 30
NLAT = 64
NLON = 1024


def level_field(base_key):
    key_depth, key_coast, key_tiles = jax.random.split(jax.random.fold_in(base_key, 7), 3)
    depth = jax.random.randint(key_depth, (NLAT, NLON), 4, NZ + 1)
    coast = jax.random.randint(key_coast, (NLAT, NLON), 0, 5) == 0
    tiles = jax.random.randint(key_tiles, (NLAT // CLAT, NLON // CLON), 0, 8) == 0
    tiles = jnp.repeat(jnp.repeat(tiles, CLAT, 0), CLON, 1)
    row_index = jnp.arange(NLAT)[:, None]
    edges = (row_index == 0) | (row_index == NLAT - 1)
    return jnp.where(coast | tiles | edges, 0, depth).astype(jnp.int32)


def velocity_field(base_key, shift_axis, noise_tag):
    counts = level_field(base_key)
    face_count = jnp.minimum(counts, jnp.roll(counts, -1, shift_axis))
    wet_mask = jnp.arange(NZ)[:, None, None] < face_count[None]
    noise_key = jax.random.fold_in(base_key, noise_tag)
    values = jax.random.normal(noise_key, (NZ, NLAT, NLON), jnp.float32)
    return jnp.where(wet_mask, values, 0.0).astype(jnp.float32)


def draw_level_count(key, part):
    return level_field(key)


def draw_zonal_velocity(key, part):
    return velocity_field(key, -1, 11)


def draw_northward_velocity(key, part):
    return velocity_field(key, -2, 13)


def shard_levels(key, shape, pieces, smallest, top_value):
    def one(axis_at, blocks):
        heights = jax.random.uniform(jax.random.fold_in(jax.random.fold_in(key, 6), axis_at), (blocks,), jnp.float32, smallest / len(pieces), top_value / len(pieces))
        return jnp.repeat(jnp.exp(heights), shape[axis_at] // blocks).reshape((-1,) + (1,) * (len(shape) - axis_at - 1))

    loudness = one(*pieces[0])
    for cut in pieces[1:]:
        loudness = loudness * one(*cut)
    return loudness


def normal_values(own_key, extent, deviation, most, shards=(), kind=jnp.bfloat16):
    entries = jax.random.normal(own_key, extent, jnp.float32) * deviation
    if len(shards) > 0:
        entries = shard_levels(own_key, extent, shards, -0.22, 0.18) * entries
    return jnp.clip(entries, min=-most, max=most).astype(kind)


def setup_inputs(seed: int = 0) -> dict:
    keys = jax.random.split(jax.random.key(seed), 8)
    zonal_velocity = draw_zonal_velocity(jax.random.fold_in(keys[7], 71), 0)
    northward_velocity = draw_northward_velocity(jax.random.fold_in(keys[7], 71), 0)
    level_count = draw_level_count(jax.random.fold_in(keys[7], 71), 0)
    surface_height = normal_values(keys[3], (NLAT, NLON), 0.5, 4.0, ((0, 4), (1, 8)), jnp.float32)
    zonal_transport = normal_values(keys[4], (NLAT, NLON), 0.5, 4.0, ((0, 4), (1, 8)), jnp.float32)
    northward_transport = normal_values(keys[5], (NLAT, NLON), 0.5, 4.0, ((0, 4), (1, 8)), jnp.float32)
    thickness = jnp.clip(jnp.exp(jax.random.uniform(keys[6], (NZ,), jnp.float32, math.log(0.015), math.log(0.06))), 0.015, 0.06)
    return {"zonal_velocity": zonal_velocity, "northward_velocity": northward_velocity, "level_count": level_count, "surface_height": surface_height, "zonal_transport": zonal_transport, "northward_transport": northward_transport, "thickness": thickness}


viscosity = 0.01
timestep = 0.35


def eastward(grid_field):
    return jnp.roll(grid_field, -1, -1)


def westward(grid_field):
    return jnp.roll(grid_field, 1, -1)


def northward(grid_field):
    return jnp.roll(grid_field, -1, -2)


def southward(grid_field):
    return jnp.roll(grid_field, 1, -2)


def laplace(grid_field):
    return eastward(grid_field) + westward(grid_field) + northward(grid_field) + southward(grid_field) - 4.0 * grid_field


def substep(height, flux_east, flux_north, depth_east, depth_north, force_east, force_north):
    spread = flux_east - jnp.roll(flux_east, 1, -1) + flux_north - jnp.roll(flux_north, 1, -2)
    height = height - timestep * spread
    flux_east = flux_east - timestep * depth_east * (jnp.roll(height, -1, -1) - height) + timestep * force_east
    flux_north = flux_north - timestep * depth_north * (jnp.roll(height, -1, -2) - height) + timestep * force_north
    return height, flux_east, flux_north


def reference(zonal_velocity, northward_velocity, level_count, surface_height, zonal_transport, northward_transport, thickness):
    face_east = jnp.minimum(level_count, eastward(level_count))
    face_north = jnp.minimum(level_count, northward(level_count))
    layers = jnp.arange(NZ, dtype=jnp.int32)

    def tendency(grid_field, face_count, level_index):
        wet_mask = (level_index < face_count).astype(jnp.float32)
        return -viscosity * wet_mask * laplace(wet_mask * laplace(grid_field)), wet_mask

    def level_sums(running, inputs):
        zonal_level, north_level, layer_depth, level_index = inputs
        tend_east, wet_east = tendency(zonal_level, face_east, level_index)
        tend_north, wet_north = tendency(north_level, face_north, level_index)
        depth_east, depth_north, force_east, force_north, column_east, column_north = running
        return (depth_east + layer_depth * wet_east,
                depth_north + layer_depth * wet_north,
                force_east + layer_depth * tend_east,
                force_north + layer_depth * tend_north,
                column_east + layer_depth * (zonal_level + tend_east),
                column_north + layer_depth * (north_level + tend_north)), None

    zeros = jnp.zeros(level_count.shape, jnp.float32)
    sums, unused = lax.scan(level_sums, (zeros, zeros, zeros, zeros, zeros, zeros),
                            (zonal_velocity, northward_velocity, thickness, layers))
    depth_east, depth_north, force_east, force_north, column_east, column_north = sums
    force_east = force_east / (NSUB * timestep)
    force_north = force_north / (NSUB * timestep)
    open_east = (face_east > 0).astype(jnp.float32)
    open_north = (face_north > 0).astype(jnp.float32)
    height = surface_height
    flux_east = open_east * zonal_transport
    flux_north = open_north * northward_transport
    total_east = zeros
    total_north = zeros
    for repeat in range(NSUB):
        height, flux_east, flux_north = substep(height, flux_east, flux_north, depth_east, depth_north, force_east, force_north)
        total_east = total_east + flux_east
        total_north = total_north + flux_north
    mean_east = total_east / NSUB
    mean_north = total_north / NSUB
    shift_east = (mean_east - column_east) / (depth_east + 1.0 - open_east)
    shift_north = (mean_north - column_north) / (depth_north + 1.0 - open_north)

    def level_after(inputs):
        zonal_level, north_level, level_index = inputs
        tend_east, wet_east = tendency(zonal_level, face_east, level_index)
        tend_north, wet_north = tendency(north_level, face_north, level_index)
        return (wet_east * ((zonal_level + tend_east) + shift_east),
                wet_north * ((north_level + tend_north) + shift_north))

    zonal_after, northward_after = lax.map(level_after, (zonal_velocity, northward_velocity, layers))
    return (zonal_after, northward_after, height, mean_east, mean_north)
```

```python
import functools

import jax
import jax.numpy as jnp
from jax import lax
from jax.experimental import pallas as pl
from jax.experimental.pallas import tpu as pltpu
from jax.sharding import PartitionSpec as P

NSUB = 30
VISCOSITY = 0.01
TIMESTEP = 0.35
LANES = 128
GROUP = 4
PER_TILE = LANES // GROUP
MESH = pl.DeviceIdType.MESH


def lane_of(x):
    return lax.broadcasted_iota(jnp.int32, x.shape, 1)


def sub_of(x):
    return lax.broadcasted_iota(jnp.int32, x.shape, 0)


def lanes(x, shift):
    return pltpu.roll(x, shift % LANES, 1)


def up(x):
    return pltpu.roll(x, x.shape[0] - 1, 0)


def down(x):
    return pltpu.roll(x, 1, 0)


def east(main, side):
    a, b = lanes(main, -1), lanes(side, -1)
    last = lane_of(main) == LANES - 1
    return jnp.where(last, b, a), jnp.where(last, a, b)


def west(main, side):
    a, b = lanes(main, 1), lanes(side, 1)
    first = lane_of(main) == 0
    return jnp.where(first, b, a), jnp.where(first, a, b)


def segments(layers):
    found, q = [], 0
    for field in range(2):
        k = 0
        while k < layers:
            n = min(layers - k, PER_TILE - q % PER_TILE)
            found.append((field, k, n, q // PER_TILE, q % PER_TILE))
            k, q = k + n, q + n
    return found


def kernel(
    nlon, nlat, tiles, centre,
    thick, ve, vn, cnt, height, te, tn,
    oe, on, oh, ome, omn,
    rows_e, rows_n, packed, from_east, from_west, corner, corner_count, inject,
    state, state_side, state_east, state_west,
    count, count_side, count_east, count_west,
    force, force_side, force_east, force_west,
    send, recv,
):
    layers, r, _ = ve.shape
    lon, lat = lax.axis_index("lon"), lax.axis_index("lat")
    offsets = [o for o in range(centre - tiles + 1, centre + 1) if o != 0]

    def device(dx, dy):
        return {"lon": lax.rem(lon + nlon + dx, nlon), "lat": lax.rem(lat + nlat + dy, nlat)}

    partners = [(1, 0), (-1, 0)] + [(0, o) for o in offsets]
    partners += [(dx, dy) for dx in (1, -1) for dy in (1, -1)]
    barrier = pltpu.get_barrier_semaphore()
    for dx, dy in partners:
        pl.semaphore_signal(barrier, inc=1, device_id=device(dx, dy), device_id_type=MESH)

    used = [0]
    started = []

    def push(src, dst, dx, dy):
        i = used[0]
        used[0] += 1
        c = pltpu.make_async_remote_copy(
            src_ref=src, dst_ref=dst, send_sem=send.at[i], recv_sem=recv.at[i],
            device_id=device(dx, dy), device_id_type=MESH)
        c.start()
        started.append(c)
        return c

    ntiles = packed.shape[0]
    for t in range(ntiles):
        acc = jnp.zeros((r, LANES), jnp.float32)
        for field, k0, n, tile, m0 in segments(layers):
            if tile != t:
                continue
            v = (ve, vn)[field]

            def put(i, acc, v=v, k0=k0, m0=m0):
                m = m0 + i
                x = pltpu.roll(v[k0 + i], GROUP * m + 2 - LANES * ((GROUP * m + 2) // LANES), 1)
                return jnp.where(lane_of(x) // GROUP == m, x, acc)

            acc = lax.fori_loop(0, n, put, acc, unroll=4)
        packed[t] = acc
    pl.semaphore_wait(barrier, len(partners))

    lon_v = [push(packed, from_west, 1, 0), push(packed, from_east, -1, 0)]
    diag = [(-1, -1, 0), (-1, 1, 1), (1, -1, 2), (1, 1, 3)]
    half = r // 2
    diag_v, diag_c = [], []
    for dx, dy, slot in diag:
        part = pl.ds(0, 8) if dy < 0 else pl.ds(r - 8, 8)
        diag_v.append(push(packed.at[:, part], corner.at[slot], dx, dy))
        diag_c.append(push(cnt.at[part], corner_count.at[slot], dx, dy))
    lon_c = [push(cnt, count_west, 1, 0), push(cnt, count_east, -1, 0)]
    lat_v = []
    for v, buf in ((ve, rows_e), (vn, rows_n)):
        lat_v.append(push(v.at[:, pl.ds(0, 2)], buf.at[:, pl.ds(0, 2)], 0, -1))
        lat_v.append(push(v.at[:, pl.ds(r - 2, 2)], buf.at[:, pl.ds(6, 2)], 0, 1))
    lat_c = [push(cnt, count.at[centre - o], 0, o) for o in offsets]
    fields = (height, te, tn)
    lon_s = []
    for i, f in enumerate(fields):
        lon_s.append(push(f, state_west.at[i], 1, 0))
        lon_s.append(push(f, state_east.at[i], -1, 0))
    lat_s = [push(f, state.at[centre - o, i], 0, o) for i, f in enumerate(fields) for o in offsets]
    count[centre] = cnt[...]
    for i, f in enumerate(fields):
        state[centre, i] = f[...]

    right = lax.broadcasted_iota(jnp.int32, (r, LANES), 1) < LANES // 2
    for c in lon_v + diag_v + diag_c + lon_c + lat_v + lat_c:
        c.wait_recv()

    low = lax.broadcasted_iota(jnp.int32, (8, LANES), 0) < 4

    def ring(x, north, south):
        return jnp.concatenate([x, jnp.where(low, north, south)], 0)

    c24 = ring(cnt[...], count[(centre + 1) % tiles, 0:8], count[(centre - 1) % tiles, r - 8:r])
    ce = ring(count_east[...], corner_count[0], corner_count[1])
    cw = ring(count_west[...], corner_count[2], corner_count[3])
    lane = lane_of(c24)
    face_e = jnp.minimum(c24, jnp.where(lane == LANES - 1, lanes(ce, -1), lanes(c24, -1)))
    face_n = jnp.minimum(c24, up(c24))

    def spread(x):
        x = jnp.where(lane < 2, x, 0)
        step = GROUP
        while step < LANES:
            x = x + lanes(x, step)
            step *= 2
        return x

    inner = spread(jnp.where(lane == 0, ce, lanes(cw, 2)))
    outer = spread(jnp.where(lane == 0, lanes(ce, -1), lanes(c24, 1)))
    edge_e = jnp.minimum(inner, outer)[:r]
    edge_n = jnp.minimum(inner, up(inner))[:r]
    slot16 = lax.broadcasted_iota(jnp.int32, (r, LANES), 1)
    place = slot16 % GROUP
    for t in range(ntiles):
        fe = ring(from_east[t], corner[0, t], corner[1, t])
        fw = ring(from_west[t], corner[2, t], corner[3, t])
        g = jnp.where(lane % GROUP == 0, lanes(fe, -2), fw)
        across = jnp.where(place == 0, lanes(fe[:r], -3), lanes(fw[:r], 1)) + lanes(packed[t], -1)
        q = t * PER_TILE + slot16 // GROUP
        k = jnp.where(q < layers, q, q - layers)
        wet = k < jnp.where(q < layers, edge_e, edge_n)
        e = jnp.where(wet, across + up(g)[:r] + down(g)[:r] - 4.0 * g[:r], 0.0)
        inject[t, 0:r] = jnp.where(place < 2, g[:r], lanes(e, 2))
        inject[t, r:r + 8] = g[r:]

    first, last = lane == 0, lane == LANES - 1
    first16, last16 = first[:r], last[:r]
    sums = []
    for field, (v, buf, face, out) in enumerate(((ve, rows_e, face_e, oe), (vn, rows_n, face_n, on))):

        def level(k, carry, field=field, v=v, buf=buf, face=face, out=out):
            total, column = carry
            q = field * layers + k
            t = q // PER_TILE
            m = q - t * PER_TILE
            own = v[k]
            x = jnp.concatenate([own, buf[k]], 0)
            j = inject[t]
            turn = LANES - 1 - GROUP * m
            turn = jnp.where(turn < 0, turn + LANES, turn)
            rim = pltpu.roll(j, turn, 1)
            rim2 = pltpu.roll(j[:r], jnp.where(turn < 2, turn + LANES - 2, turn - 2), 1)
            wet = k < face
            l1 = (jnp.where(last, rim, lanes(x, -1)) + jnp.where(first, rim, lanes(x, 1))
                  + up(x) + down(x) - 4.0 * x)
            l1 = jnp.where(wet, l1, 0.0)
            mid = l1[:r]
            l2 = (jnp.where(last16, rim2, lanes(mid, -1)) + jnp.where(first16, rim2, lanes(mid, 1))
                  + up(l1)[:r] + down(l1)[:r] - 4.0 * mid)
            tend = jnp.where(wet[:r], -VISCOSITY * l2, 0.0)
            after = own + tend
            out[k] = after
            return total + thick[k] * tend, column + thick[k] * after

        zero = jnp.zeros((r, LANES), jnp.float32)
        sums.append(lax.fori_loop(0, layers, level, (zero, zero), unroll=4))
    (sum_e, column_e), (sum_n, column_n) = sums
    force[centre, 0] = sum_e * (TIMESTEP / NSUB)
    force[centre, 1] = sum_n * (TIMESTEP / NSUB)
    lon_f = [push(force.at[centre], force_west, 1, 0), push(force.at[centre], force_east, -1, 0)]
    lat_f = [push(force.at[centre], force.at[centre - o], 0, o) for o in offsets]

    for c in lon_s:
        c.wait_recv()
    count_side[centre] = jnp.where(right, count_east[...], count_west[...])
    for i in range(3):
        state_side[centre, i] = jnp.where(right, state_east[i], state_west[i])
    side_c = [push(count_side.at[centre], count_side.at[centre - o], 0, o) for o in offsets]
    side_s = [push(state_side.at[centre], state_side.at[centre - o], 0, o) for o in offsets]

    for c in side_c + side_s + lat_s:
        c.wait_recv()
    span = tiles * r
    cm, cs = count[...].reshape(span, LANES), count_side[...].reshape(span, LANES)

    def deepen(k, carry):
        dm, ds = carry
        return jnp.where(k < cm, dm + thick[k], dm), jnp.where(k < cs, ds + thick[k], ds)

    zero = jnp.zeros((span, LANES), jnp.float32)
    dm, ds = lax.fori_loop(0, layers, deepen, (zero, zero), unroll=4)
    em, es = east(dm, ds)
    em, es = jnp.minimum(dm, em), jnp.minimum(ds, es)
    nm, ns = jnp.minimum(dm, up(dm)), jnp.minimum(ds, up(ds))

    def take(buf, i):
        return buf[:, i].reshape(span, LANES)

    def gate(depth, flux):
        return jnp.where(depth > 0, TIMESTEP * flux, 0.0)

    own = slice(centre * r, centre * r + r)
    depth_e, depth_n = em[own], nm[own]
    now = [take(state, 0), take(state_side, 0), gate(em, take(state, 1)), gate(es, take(state_side, 1)),
           gate(nm, take(state, 2)), gate(ns, take(state_side, 2))]
    square = TIMESTEP * TIMESTEP
    fixed = [square * em, square * es, square * nm, square * ns]

    for c in lon_f:
        c.wait_recv()
    for i in range(2):
        force_side[centre, i] = jnp.where(right, force_east[i], force_west[i])
    side_f = [push(force_side.at[centre], force_side.at[centre - o], 0, o) for o in offsets]
    for c in lat_f + side_f:
        c.wait_recv()
    fixed += [take(force, 0), take(force_side, 0), take(force, 1), take(force_side, 1)]

    zero = jnp.zeros((r, LANES), jnp.float32)
    totals = (zero, zero)
    plan = [(NSUB, span, 0)]
    if tiles >= 3:
        plan = [(NSUB - 16, span, 0), (8, 3 * r, (centre - 1) * r), (8, 2 * r, centre * r - half)]
    base = 0
    for steps, size, start in plan:
        cut = slice(start - base, start - base + size)
        now = [x[cut] for x in now]
        fixed = [x[cut] for x in fixed]
        base = start
        mine = slice(centre * r - base, centre * r - base + r)
        aem, aes, anm, ans, bem, bes, bnm, bns = fixed

        def step(_, carry, mine=mine, aem=aem, aes=aes, anm=anm, ans=ans, bem=bem, bes=bes, bnm=bnm, bns=bns):
            hm, hs, xm, xs, ym, ys, tot_e, tot_n = carry
            wm, ws = west(xm, xs)
            hm = hm - ((xm - wm) + (ym - down(ym)))
            hs = hs - ((xs - ws) + (ys - down(ys)))
            gm, gs = east(hm, hs)
            xm = xm - aem * (gm - hm) + bem
            xs = xs - aes * (gs - hs) + bes
            ym = ym - anm * (up(hm) - hm) + bnm
            ys = ys - ans * (up(hs) - hs) + bns
            return hm, hs, xm, xs, ym, ys, tot_e + xm[mine], tot_n + ym[mine]

        *now, tot_e, tot_n = lax.fori_loop(0, steps, step, (*now, *totals))
        totals = (tot_e, tot_n)
    oh[...] = now[0][mine]
    mean_e = totals[0] / (NSUB * TIMESTEP)
    mean_n = totals[1] / (NSUB * TIMESTEP)
    ome[...] = mean_e
    omn[...] = mean_n
    one = jnp.ones((r, LANES), jnp.float32)
    shift_e = (mean_e - column_e) / (depth_e + jnp.where(depth_e > 0, 0.0, one))
    shift_n = (mean_n - column_n) / (depth_n + jnp.where(depth_n > 0, 0.0, one))
    own_e, own_n = face_e[:r], face_n[:r]

    def finish(k, _):
        oe[k] = jnp.where(k < own_e, oe[k] + shift_e, 0.0)
        on[k] = jnp.where(k < own_n, on[k] + shift_n, 0.0)
        return 0

    lax.fori_loop(0, layers, finish, 0, unroll=4)
    for c in started:
        c.wait_send()


def solution(mesh):
    nlon, nlat = mesh.shape["lon"], mesh.shape["lat"]

    def shards(ve, vn, cnt, height, te, tn, thick):
        layers, r, width = ve.shape
        reach = -(-NSUB // r)
        tiles = min(nlat, 2 * reach + 1)
        centre = tiles // 2
        ntiles = -(-2 * layers // PER_TILE)
        f32, i32 = jnp.float32, jnp.int32
        tile = (r, width)
        vm = pltpu.VMEM
        vspec = pl.BlockSpec(memory_space=pltpu.VMEM)
        copies = 2 + 8 + 2 + 4 + 6 + 2 + 8 * (tiles - 1)
        return pl.pallas_call(
            functools.partial(kernel, nlon, nlat, tiles, centre),
            out_shape=(
                jax.ShapeDtypeStruct(ve.shape, f32),
                jax.ShapeDtypeStruct(ve.shape, f32),
                jax.ShapeDtypeStruct(tile, f32),
                jax.ShapeDtypeStruct(tile, f32),
                jax.ShapeDtypeStruct(tile, f32),
            ),
            in_specs=[pl.BlockSpec(memory_space=pltpu.SMEM)] + [vspec] * 6,
            out_specs=[vspec] * 5,
            scratch_shapes=[
                vm((layers, 8, width), f32),
                vm((layers, 8, width), f32),
                vm((ntiles, *tile), f32),
                vm((ntiles, *tile), f32),
                vm((ntiles, *tile), f32),
                vm((4, ntiles, 8, width), f32),
                vm((4, 8, width), i32),
                vm((ntiles, r + 8, width), f32),
                vm((tiles, 3, *tile), f32),
                vm((tiles, 3, *tile), f32),
                vm((3, *tile), f32),
                vm((3, *tile), f32),
                vm((tiles, *tile), i32),
                vm((tiles, *tile), i32),
                vm(tile, i32),
                vm(tile, i32),
                vm((tiles, 2, *tile), f32),
                vm((tiles, 2, *tile), f32),
                vm((2, *tile), f32),
                vm((2, *tile), f32),
                pltpu.SemaphoreType.DMA((copies,)),
                pltpu.SemaphoreType.DMA((copies,)),
            ],
            compiler_params=pltpu.CompilerParams(collective_id=0, has_side_effects=True),
        )(thick, ve, vn, cnt, height, te, tn)

    level = P(None, "lat", "lon")
    flat = P("lat", "lon")
    return jax.shard_map(
        shards,
        mesh=mesh,
        in_specs=(level, level, flat, flat, flat, flat, P()),
        out_specs=(level, level, flat, flat, flat),
        check_vma=False,
    )
```

```python
import functools

import jax
import jax.numpy as jnp
from jax import lax
from jax.experimental import pallas as pl
from jax.experimental.pallas import tpu as pltpu
from jax.sharding import PartitionSpec as P

NSUB = 30
VISCOSITY = 0.01
TIMESTEP = 0.35
LANES = 128
GROUP = 4
PER_TILE = LANES // GROUP
MESH = pl.DeviceIdType.MESH


def lane_of(x):
    return lax.broadcasted_iota(jnp.int32, x.shape, 1)


def sub_of(x):
    return lax.broadcasted_iota(jnp.int32, x.shape, 0)


def lanes(x, shift):
    return pltpu.roll(x, shift % LANES, 1)


def up(x):
    return pltpu.roll(x, x.shape[0] - 1, 0)


def down(x):
    return pltpu.roll(x, 1, 0)


def east(main, side):
    a, b = lanes(main, -1), lanes(side, -1)
    last = lane_of(main) == LANES - 1
    return jnp.where(last, b, a), jnp.where(last, a, b)


def west(main, side):
    a, b = lanes(main, 1), lanes(side, 1)
    first = lane_of(main) == 0
    return jnp.where(first, b, a), jnp.where(first, a, b)


def segments(layers):
    found, q = [], 0
    for field in range(2):
        k = 0
        while k < layers:
            n = min(layers - k, PER_TILE - q % PER_TILE)
            found.append((field, k, n, q // PER_TILE, q % PER_TILE))
            k, q = k + n, q + n
    return found


def kernel(
    nlon, nlat, tiles, centre,
    thick_hbm, ve_hbm, vn_hbm, cnt_hbm, height_hbm, te_hbm, tn_hbm,
    oe, on, small,
    thick, ve, vn, cnt, height, te, tn, loads,
    rows_e, rows_n, packed, from_east, from_west, corner, corner_count, inject,
    state, state_side, state_east, state_west,
    count, count_side, count_east, count_west,
    force, force_side, force_east, force_west,
    send, recv,
):
    layers, r, _ = ve.shape
    lon, lat = lax.axis_index("lon"), lax.axis_index("lat")
    offsets = [o for o in range(centre - tiles + 1, centre + 1) if o != 0]

    def device(dx, dy):
        return {"lon": lax.rem(lon + nlon + dx, nlon), "lat": lax.rem(lat + nlat + dy, nlat)}

    partners = [(1, 0), (-1, 0)] + [(0, o) for o in offsets]
    partners += [(dx, dy) for dx in (1, -1) for dy in (1, -1)]
    barrier = pltpu.get_barrier_semaphore()
    for dx, dy in partners:
        pl.semaphore_signal(barrier, inc=1, device_id=device(dx, dy), device_id_type=MESH)

    fetched = []
    for i, (far, near) in enumerate((
        (ve_hbm, ve), (vn_hbm, vn), (cnt_hbm, cnt), (height_hbm, height), (te_hbm, te), (tn_hbm, tn),
        (thick_hbm, thick),
    )):
        fetched.append(pltpu.make_async_copy(far, near, loads.at[i]))
        fetched[-1].start()

    used = [0]
    started = []

    def push(src, dst, dx, dy):
        i = used[0]
        used[0] += 1
        c = pltpu.make_async_remote_copy(
            src_ref=src, dst_ref=dst, send_sem=send.at[i], recv_sem=recv.at[i],
            device_id=device(dx, dy), device_id_type=MESH)
        c.start()
        started.append(c)
        return c

    for c in fetched:
        c.wait()

    ntiles = packed.shape[0]
    for t in range(ntiles):
        acc = jnp.zeros((r, LANES), jnp.float32)
        for field, k0, n, tile, m0 in segments(layers):
            if tile != t:
                continue
            v = (ve, vn)[field]

            def put(i, acc, v=v, k0=k0, m0=m0):
                m = m0 + i
                x = pltpu.roll(v[k0 + i], GROUP * m + 2 - LANES * ((GROUP * m + 2) // LANES), 1)
                return jnp.where(lane_of(x) // GROUP == m, x, acc)

            acc = lax.fori_loop(0, n, put, acc, unroll=4)
        packed[t] = acc
    pl.semaphore_wait(barrier, len(partners))

    lon_v = [push(packed, from_west, 1, 0), push(packed, from_east, -1, 0)]
    diag = [(-1, -1, 0), (-1, 1, 1), (1, -1, 2), (1, 1, 3)]
    half = r // 2
    diag_v, diag_c = [], []
    for dx, dy, slot in diag:
        part = pl.ds(0, 8) if dy < 0 else pl.ds(r - 8, 8)
        diag_v.append(push(packed.at[:, part], corner.at[slot], dx, dy))
        diag_c.append(push(cnt.at[part], corner_count.at[slot], dx, dy))
    lon_c = [push(cnt, count_west, 1, 0), push(cnt, count_east, -1, 0)]
    lat_v = []
    for v, buf in ((ve, rows_e), (vn, rows_n)):
        lat_v.append(push(v.at[:, pl.ds(0, 2)], buf.at[:, pl.ds(0, 2)], 0, -1))
        lat_v.append(push(v.at[:, pl.ds(r - 2, 2)], buf.at[:, pl.ds(6, 2)], 0, 1))
    lat_c = [push(cnt, count.at[centre - o], 0, o) for o in offsets]
    fields = (height, te, tn)
    lon_s = []
    for i, f in enumerate(fields):
        lon_s.append(push(f, state_west.at[i], 1, 0))
        lon_s.append(push(f, state_east.at[i], -1, 0))
    lat_s = [push(f, state.at[centre - o, i], 0, o) for i, f in enumerate(fields) for o in offsets]
    count[centre] = cnt[...]
    for i, f in enumerate(fields):
        state[centre, i] = f[...]

    right = lax.broadcasted_iota(jnp.int32, (r, LANES), 1) < LANES // 2
    for c in lon_v + diag_v + diag_c + lon_c + lat_v + lat_c:
        c.wait_recv()

    low = lax.broadcasted_iota(jnp.int32, (8, LANES), 0) < 4

    def ring(x, north, south):
        return jnp.concatenate([x, jnp.where(low, north, south)], 0)

    c24 = ring(cnt[...], count[(centre + 1) % tiles, 0:8], count[(centre - 1) % tiles, r - 8:r])
    ce = ring(count_east[...], corner_count[0], corner_count[1])
    cw = ring(count_west[...], corner_count[2], corner_count[3])
    lane = lane_of(c24)
    face_e = jnp.minimum(c24, jnp.where(lane == LANES - 1, lanes(ce, -1), lanes(c24, -1)))
    face_n = jnp.minimum(c24, up(c24))

    def spread(x):
        x = jnp.where(lane < 2, x, 0)
        step = GROUP
        while step < LANES:
            x = x + lanes(x, step)
            step *= 2
        return x

    inner = spread(jnp.where(lane == 0, ce, lanes(cw, 2)))
    outer = spread(jnp.where(lane == 0, lanes(ce, -1), lanes(c24, 1)))
    edge_e = jnp.minimum(inner, outer)[:r]
    edge_n = jnp.minimum(inner, up(inner))[:r]
    slot16 = lax.broadcasted_iota(jnp.int32, (r, LANES), 1)
    place = slot16 % GROUP
    for t in range(ntiles):
        fe = ring(from_east[t], corner[0, t], corner[1, t])
        fw = ring(from_west[t], corner[2, t], corner[3, t])
        g = jnp.where(lane % GROUP == 0, lanes(fe, -2), fw)
        across = jnp.where(place == 0, lanes(fe[:r], -3), lanes(fw[:r], 1)) + lanes(packed[t], -1)
        q = t * PER_TILE + slot16 // GROUP
        k = jnp.where(q < layers, q, q - layers)
        wet = k < jnp.where(q < layers, edge_e, edge_n)
        e = jnp.where(wet, across + up(g)[:r] + down(g)[:r] - 4.0 * g[:r], 0.0)
        inject[t, 0:r] = jnp.where(place < 2, g[:r], lanes(e, 2))
        inject[t, r:r + 8] = g[r:]

    first, last = lane == 0, lane == LANES - 1
    first16, last16 = first[:r], last[:r]
    sums = []
    for field, (v, buf, face, out) in enumerate(((ve, rows_e, face_e, oe), (vn, rows_n, face_n, on))):

        def level(k, carry, field=field, v=v, buf=buf, face=face, out=out):
            total, column = carry
            q = field * layers + k
            t = q // PER_TILE
            m = q - t * PER_TILE
            own = v[k]
            x = jnp.concatenate([own, buf[k]], 0)
            j = inject[t]
            turn = LANES - 1 - GROUP * m
            turn = jnp.where(turn < 0, turn + LANES, turn)
            rim = pltpu.roll(j, turn, 1)
            rim2 = pltpu.roll(j[:r], jnp.where(turn < 2, turn + LANES - 2, turn - 2), 1)
            wet = k < face
            l1 = (jnp.where(last, rim, lanes(x, -1)) + jnp.where(first, rim, lanes(x, 1))
                  + up(x) + down(x) - 4.0 * x)
            l1 = jnp.where(wet, l1, 0.0)
            mid = l1[:r]
            l2 = (jnp.where(last16, rim2, lanes(mid, -1)) + jnp.where(first16, rim2, lanes(mid, 1))
                  + up(l1)[:r] + down(l1)[:r] - 4.0 * mid)
            tend = jnp.where(wet[:r], -VISCOSITY * l2, 0.0)
            after = own + tend
            out[k] = after
            return total + thick[k] * tend, column + thick[k] * after

        zero = jnp.zeros((r, LANES), jnp.float32)
        sums.append(lax.fori_loop(0, layers, level, (zero, zero), unroll=4))
    (sum_e, column_e), (sum_n, column_n) = sums
    force[centre, 0] = sum_e * (TIMESTEP / NSUB)
    force[centre, 1] = sum_n * (TIMESTEP / NSUB)
    lon_f = [push(force.at[centre], force_west, 1, 0), push(force.at[centre], force_east, -1, 0)]
    lat_f = [push(force.at[centre], force.at[centre - o], 0, o) for o in offsets]

    for c in lon_s:
        c.wait_recv()
    count_side[centre] = jnp.where(right, count_east[...], count_west[...])
    for i in range(3):
        state_side[centre, i] = jnp.where(right, state_east[i], state_west[i])
    side_c = [push(count_side.at[centre], count_side.at[centre - o], 0, o) for o in offsets]
    side_s = [push(state_side.at[centre], state_side.at[centre - o], 0, o) for o in offsets]

    for c in side_c + side_s + lat_s:
        c.wait_recv()
    span = tiles * r
    cm, cs = count[...].reshape(span, LANES), count_side[...].reshape(span, LANES)

    def deepen(k, carry):
        dm, ds = carry
        return jnp.where(k < cm, dm + thick[k], dm), jnp.where(k < cs, ds + thick[k], ds)

    zero = jnp.zeros((span, LANES), jnp.float32)
    dm, ds = lax.fori_loop(0, layers, deepen, (zero, zero), unroll=4)
    em, es = east(dm, ds)
    em, es = jnp.minimum(dm, em), jnp.minimum(ds, es)
    nm, ns = jnp.minimum(dm, up(dm)), jnp.minimum(ds, up(ds))

    def take(buf, i):
        return buf[:, i].reshape(span, LANES)

    def gate(depth, flux):
        return jnp.where(depth > 0, TIMESTEP * flux, 0.0)

    own = slice(centre * r, centre * r + r)
    depth_e, depth_n = em[own], nm[own]
    now = [take(state, 0), take(state_side, 0), gate(em, take(state, 1)), gate(es, take(state_side, 1)),
           gate(nm, take(state, 2)), gate(ns, take(state_side, 2))]
    square = TIMESTEP * TIMESTEP
    fixed = [square * em, square * es, square * nm, square * ns]

    for c in lon_f:
        c.wait_recv()
    for i in range(2):
        force_side[centre, i] = jnp.where(right, force_east[i], force_west[i])
    side_f = [push(force_side.at[centre], force_side.at[centre - o], 0, o) for o in offsets]
    for c in lat_f + side_f:
        c.wait_recv()
    fixed += [take(force, 0), take(force_side, 0), take(force, 1), take(force_side, 1)]

    zero = jnp.zeros((r, LANES), jnp.float32)
    totals = (zero, zero)
    plan = [(NSUB, span, 0)]
    if tiles >= 3:
        plan = [(NSUB - 16, span, 0), (8, 3 * r, (centre - 1) * r), (8, 2 * r, centre * r - half)]
    base = 0
    for steps, size, start in plan:
        cut = slice(start - base, start - base + size)
        now = [x[cut] for x in now]
        fixed = [x[cut] for x in fixed]
        base = start
        mine = slice(centre * r - base, centre * r - base + r)
        aem, aes, anm, ans, bem, bes, bnm, bns = fixed

        def step(_, carry, mine=mine, aem=aem, aes=aes, anm=anm, ans=ans, bem=bem, bes=bes, bnm=bnm, bns=bns):
            hm, hs, xm, xs, ym, ys, tot_e, tot_n = carry
            wm, ws = west(xm, xs)
            hm = hm - ((xm - wm) + (ym - down(ym)))
            hs = hs - ((xs - ws) + (ys - down(ys)))
            gm, gs = east(hm, hs)
            xm = xm - aem * (gm - hm) + bem
            xs = xs - aes * (gs - hs) + bes
            ym = ym - anm * (up(hm) - hm) + bnm
            ys = ys - ans * (up(hs) - hs) + bns
            return hm, hs, xm, xs, ym, ys, tot_e + xm[mine], tot_n + ym[mine]

        *now, tot_e, tot_n = lax.fori_loop(0, steps, step, (*now, *totals))
        totals = (tot_e, tot_n)
    mean_e = totals[0] / (NSUB * TIMESTEP)
    mean_n = totals[1] / (NSUB * TIMESTEP)
    one = jnp.ones((r, LANES), jnp.float32)
    small[0] = now[0][mine]
    small[1] = mean_e
    small[2] = mean_n
    small[3] = (mean_e - column_e) / (depth_e + jnp.where(depth_e > 0, 0.0, one))
    small[4] = (mean_n - column_n) / (depth_n + jnp.where(depth_n > 0, 0.0, one))
    small[5] = face_e[:r].astype(jnp.float32)
    small[6] = face_n[:r].astype(jnp.float32)
    for c in started:
        c.wait_send()


def finish(after_e, after_n, small, oe, on, oh, ome, omn):
    oh[...] = small[0]
    ome[...] = small[1]
    omn[...] = small[2]
    face_e, face_n = small[5], small[6]
    shift_e, shift_n = small[3], small[4]

    def level(k, _):
        depth = k.astype(jnp.float32)
        oe[k] = jnp.where(depth < face_e, after_e[k] + shift_e, 0.0)
        on[k] = jnp.where(depth < face_n, after_n[k] + shift_n, 0.0)
        return 0

    lax.fori_loop(0, after_e.shape[0], level, 0, unroll=4)


def solution(mesh):
    nlon, nlat = mesh.shape["lon"], mesh.shape["lat"]

    def shards(ve, vn, cnt, height, te, tn, thick):
        layers, r, width = ve.shape
        reach = -(-NSUB // r)
        tiles = min(nlat, 2 * reach + 1)
        centre = tiles // 2
        ntiles = -(-2 * layers // PER_TILE)
        f32, i32 = jnp.float32, jnp.int32
        tile = (r, width)
        vm = pltpu.VMEM
        vspec = pl.BlockSpec(memory_space=pltpu.VMEM)
        copies = 2 + 8 + 2 + 4 + 6 + 2 + 8 * (tiles - 1)
        after_e, after_n, small = pl.pallas_call(
            functools.partial(kernel, nlon, nlat, tiles, centre),
            out_shape=(
                jax.ShapeDtypeStruct(ve.shape, f32),
                jax.ShapeDtypeStruct(ve.shape, f32),
                jax.ShapeDtypeStruct((7, *tile), f32),
            ),
            in_specs=[pl.BlockSpec(memory_space=pltpu.HBM)] * 7,
            out_specs=[vspec] * 3,
            scratch_shapes=[
                pltpu.SMEM((layers,), f32),
                vm(ve.shape, f32),
                vm(ve.shape, f32),
                vm(tile, i32),
                vm(tile, f32),
                vm(tile, f32),
                vm(tile, f32),
                pltpu.SemaphoreType.DMA((7,)),
                vm((layers, 8, width), f32),
                vm((layers, 8, width), f32),
                vm((ntiles, *tile), f32),
                vm((ntiles, *tile), f32),
                vm((ntiles, *tile), f32),
                vm((4, ntiles, 8, width), f32),
                vm((4, 8, width), i32),
                vm((ntiles, r + 8, width), f32),
                vm((tiles, 3, *tile), f32),
                vm((tiles, 3, *tile), f32),
                vm((3, *tile), f32),
                vm((3, *tile), f32),
                vm((tiles, *tile), i32),
                vm((tiles, *tile), i32),
                vm(tile, i32),
                vm(tile, i32),
                vm((tiles, 2, *tile), f32),
                vm((tiles, 2, *tile), f32),
                vm((2, *tile), f32),
                vm((2, *tile), f32),
                pltpu.SemaphoreType.DMA((copies,)),
                pltpu.SemaphoreType.DMA((copies,)),
            ],
            compiler_params=pltpu.CompilerParams(
                collective_id=0, has_side_effects=True, vmem_limit_bytes=16 << 20),
        )(*[pltpu.with_memory_space_constraint(x, pltpu.HBM) for x in (thick, ve, vn, cnt, height, te, tn)])
        out = jax.ShapeDtypeStruct(tile, f32)
        levels = jax.ShapeDtypeStruct(ve.shape, f32)
        return pl.pallas_call(
            finish,
            out_shape=(levels, levels, out, out, out),
            in_specs=[vspec] * 3,
            out_specs=[vspec] * 5,
            compiler_params=pltpu.CompilerParams(vmem_limit_bytes=16 << 20),
        )(after_e, after_n, small)

    level = P(None, "lat", "lon")
    flat = P("lat", "lon")
    return jax.shard_map(
        shards,
        mesh=mesh,
        in_specs=(level, level, flat, flat, flat, flat, P()),
        out_specs=(level, level, flat, flat, flat),
        check_vma=False,
    )
```

```python
import functools

import jax
import jax.numpy as jnp
from jax import lax
from jax.experimental import pallas as pl
from jax.experimental.pallas import tpu as pltpu
from jax.sharding import PartitionSpec as P

NSUB = 30
VISCOSITY = 0.01
TIMESTEP = 0.35
LANES = 128
GROUP = 4
PER_TILE = LANES // GROUP
UNROLL = 8
MESH = pl.DeviceIdType.MESH


def lane_of(x):
    return lax.broadcasted_iota(jnp.int32, x.shape, 1)


def sub_of(x):
    return lax.broadcasted_iota(jnp.int32, x.shape, 0)


def lanes(x, shift):
    return pltpu.roll(x, shift % LANES, 1)


def up(x):
    return pltpu.roll(x, x.shape[0] - 1, 0)


def down(x):
    return pltpu.roll(x, 1, 0)


def east(main, side):
    a, b = lanes(main, -1), lanes(side, -1)
    last = lane_of(main) == LANES - 1
    return jnp.where(last, b, a), jnp.where(last, a, b)


def west(main, side):
    a, b = lanes(main, 1), lanes(side, 1)
    first = lane_of(main) == 0
    return jnp.where(first, b, a), jnp.where(first, a, b)


def segments(layers):
    found, q = [], 0
    for field in range(2):
        k = 0
        while k < layers:
            n = min(layers - k, PER_TILE - q % PER_TILE)
            found.append((field, k, n, q // PER_TILE, q % PER_TILE))
            k, q = k + n, q + n
    return found


def kernel(
    nlon, nlat, tiles, centre,
    thick_hbm, ve_hbm, vn_hbm, cnt_hbm, height_hbm, te_hbm, tn_hbm,
    oe, on, small,
    thick, ve, vn, cnt, height, te, tn, loads,
    rows_e, rows_n, packed, from_east, from_west, corner, corner_count, inject,
    state, state_side, state_east, state_west,
    count, count_side, count_east, count_west,
    force, force_out, force_east, force_west,
    send, recv,
):
    layers, r, _ = ve.shape
    lon, lat = lax.axis_index("lon"), lax.axis_index("lat")
    offsets = [o for o in range(centre - tiles + 1, centre + 1) if o != 0]

    def device(dx, dy):
        return {"lon": lax.rem(lon + nlon + dx, nlon), "lat": lax.rem(lat + nlat + dy, nlat)}

    partners = [(1, 0), (-1, 0)] + [(0, o) for o in offsets]
    partners += [(dx, o) for dx in (1, -1) for o in offsets]
    barrier = pltpu.get_barrier_semaphore()
    for dx, dy in partners:
        pl.semaphore_signal(barrier, inc=1, device_id=device(dx, dy), device_id_type=MESH)

    fetched = []
    for i, (far, near) in enumerate((
        (ve_hbm, ve), (vn_hbm, vn), (cnt_hbm, cnt), (height_hbm, height), (te_hbm, te), (tn_hbm, tn),
        (thick_hbm, thick),
    )):
        fetched.append(pltpu.make_async_copy(far, near, loads.at[i]))
        fetched[-1].start()

    used = [0]
    started = []

    def push(src, dst, dx, dy):
        i = used[0]
        used[0] += 1
        c = pltpu.make_async_remote_copy(
            src_ref=src, dst_ref=dst, send_sem=send.at[i], recv_sem=recv.at[i],
            device_id=device(dx, dy), device_id_type=MESH)
        c.start()
        started.append(c)
        return c

    for c in fetched:
        c.wait()

    ntiles = packed.shape[0]
    for t in range(ntiles):
        acc = jnp.zeros((r, LANES), jnp.float32)
        for field, k0, n, tile, m0 in segments(layers):
            if tile != t:
                continue
            v = (ve, vn)[field]

            def put(i, acc, v=v, k0=k0, m0=m0):
                m = m0 + i
                x = pltpu.roll(v[k0 + i], GROUP * m + 2 - LANES * ((GROUP * m + 2) // LANES), 1)
                return jnp.where(lane_of(x) // GROUP == m, x, acc)

            acc = lax.fori_loop(0, n, put, acc, unroll=4)
        packed[t] = acc
    pl.semaphore_wait(barrier, len(partners))

    lon_v = [push(packed, from_west, 1, 0), push(packed, from_east, -1, 0)]
    diag = [(-1, -1, 0), (-1, 1, 1), (1, -1, 2), (1, 1, 3)]
    half = r // 2
    diag_v, diag_c = [], []
    for dx, dy, slot in diag:
        part = pl.ds(0, 8) if dy < 0 else pl.ds(r - 8, 8)
        diag_v.append(push(packed.at[:, part], corner.at[slot], dx, dy))
        diag_c.append(push(cnt.at[part], corner_count.at[slot], dx, dy))
    lon_c = [push(cnt, count_west, 1, 0), push(cnt, count_east, -1, 0)]
    lat_v = []
    for v, buf in ((ve, rows_e), (vn, rows_n)):
        lat_v.append(push(v.at[:, pl.ds(0, 2)], buf.at[:, pl.ds(0, 2)], 0, -1))
        lat_v.append(push(v.at[:, pl.ds(r - 2, 2)], buf.at[:, pl.ds(6, 2)], 0, 1))
    lat_c = [push(cnt, count.at[centre - o], 0, o) for o in offsets]
    fields = (height, te, tn)
    lon_s = []
    for i, f in enumerate(fields):
        lon_s.append(push(f, state_west.at[i], 1, 0))
        lon_s.append(push(f, state_east.at[i], -1, 0))
    lat_s = [push(f, state.at[centre - o, i], 0, o) for i, f in enumerate(fields) for o in offsets]
    count[centre] = cnt[...]
    for i, f in enumerate(fields):
        state[centre, i] = f[...]

    right = lax.broadcasted_iota(jnp.int32, (r, LANES), 1) < LANES // 2
    for c in lon_v + diag_v + diag_c + lon_c + lat_v + lat_c:
        c.wait_recv()

    low = lax.broadcasted_iota(jnp.int32, (8, LANES), 0) < 4

    def ring(x, north, south):
        return jnp.concatenate([x, jnp.where(low, north, south)], 0)

    c24 = ring(cnt[...], count[(centre + 1) % tiles, 0:8], count[(centre - 1) % tiles, r - 8:r])
    ce = ring(count_east[...], corner_count[0], corner_count[1])
    cw = ring(count_west[...], corner_count[2], corner_count[3])
    lane = lane_of(c24)
    face_e = jnp.minimum(c24, jnp.where(lane == LANES - 1, lanes(ce, -1), lanes(c24, -1)))
    face_n = jnp.minimum(c24, up(c24))

    def spread(x):
        x = jnp.where(lane < 2, x, 0)
        step = GROUP
        while step < LANES:
            x = x + lanes(x, step)
            step *= 2
        return x

    inner = spread(jnp.where(lane == 0, ce, lanes(cw, 2)))
    outer = spread(jnp.where(lane == 0, lanes(ce, -1), lanes(c24, 1)))
    edge_e = jnp.minimum(inner, outer)[:r]
    edge_n = jnp.minimum(inner, up(inner))[:r]
    slot16 = lax.broadcasted_iota(jnp.int32, (r, LANES), 1)
    place = slot16 % GROUP
    for t in range(ntiles):
        fe = ring(from_east[t], corner[0, t], corner[1, t])
        fw = ring(from_west[t], corner[2, t], corner[3, t])
        g = jnp.where(lane % GROUP == 0, lanes(fe, -2), fw)
        across = jnp.where(place == 0, lanes(fe[:r], -3), lanes(fw[:r], 1)) + lanes(packed[t], -1)
        q = t * PER_TILE + slot16 // GROUP
        k = jnp.where(q < layers, q, q - layers)
        wet = k < jnp.where(q < layers, edge_e, edge_n)
        e = jnp.where(wet, across + up(g)[:r] + down(g)[:r] - 4.0 * g[:r], 0.0)
        inject[t, 0:r] = jnp.where(place < 2, g[:r], lanes(e, 2))
        inject[t, r:r + 8] = g[r:]

    first, last = lane == 0, lane == LANES - 1
    first16, last16 = first[:r], last[:r]
    sums, side_c, side_s = [], [], []
    for field, (v, buf, face, out) in enumerate(((ve, rows_e, face_e, oe), (vn, rows_n, face_n, on))):

        def level(k, carry, field=field, v=v, buf=buf, face=face, out=out):
            total, column = carry
            q = field * layers + k
            t = q // PER_TILE
            m = q - t * PER_TILE
            own = v[k]
            x = jnp.concatenate([own, buf[k]], 0)
            j = inject[t]
            turn = LANES - 1 - GROUP * m
            turn = jnp.where(turn < 0, turn + LANES, turn)
            rim = pltpu.roll(j, turn, 1)
            rim2 = pltpu.roll(j[:r], jnp.where(turn < 2, turn + LANES - 2, turn - 2), 1)
            wet = k < face
            l1 = (jnp.where(last, rim, lanes(x, -1)) + jnp.where(first, rim, lanes(x, 1))
                  + up(x) + down(x) - 4.0 * x)
            l1 = jnp.where(wet, l1, 0.0)
            mid = l1[:r]
            l2 = (jnp.where(last16, rim2, lanes(mid, -1)) + jnp.where(first16, rim2, lanes(mid, 1))
                  + up(l1)[:r] + down(l1)[:r] - 4.0 * mid)
            tend = jnp.where(wet[:r], -VISCOSITY * l2, 0.0)
            after = own + tend
            out[k] = after
            return total + thick[k] * tend, column + thick[k] * after

        zero = jnp.zeros((r, LANES), jnp.float32)
        sums.append(lax.fori_loop(0, layers, level, (zero, zero), unroll=UNROLL))
        if field == 0:
            for c in lon_s:
                c.wait_recv()
            count_side[centre] = jnp.where(right, count_east[...], count_west[...])
            for i in range(3):
                state_side[centre, i] = jnp.where(right, state_east[i], state_west[i])
            side_c = [push(count_side.at[centre], count_side.at[centre - o], 0, o) for o in offsets]
            side_s = [push(state_side.at[centre], state_side.at[centre - o], 0, o) for o in offsets]
    (sum_e, column_e), (sum_n, column_n) = sums
    sum_e, sum_n = sum_e * (TIMESTEP / NSUB), sum_n * (TIMESTEP / NSUB)
    force[centre, 0] = sum_e
    force[centre, 1] = sum_n
    quarter, middle = LANES // 4, LANES // 2
    out = jnp.where(slot16 >= LANES - quarter, sum_e, lanes(sum_n, -quarter))
    force_out[0] = jnp.where(right[:8], lanes(out[:8], middle), out[8:])
    out = jnp.where(slot16 < quarter, sum_e, lanes(sum_n, quarter))
    force_out[1] = jnp.where(right[:8], out[:8], lanes(out[8:], middle))
    side_f = []
    for o in [0] + offsets:
        side_f.append(push(force_out.at[0], force_west.at[centre - o], 1, o))
        side_f.append(push(force_out.at[1], force_east.at[centre - o], -1, o))
    lat_f = [push(force.at[centre], force.at[centre - o], 0, o) for o in offsets]

    for c in side_c + side_s + lat_s:
        c.wait_recv()
    span = tiles * r
    cm, cs = count[...].reshape(span, LANES), count_side[...].reshape(span, LANES)

    def deepen(k, carry):
        dm, ds = carry
        return jnp.where(k < cm, dm + thick[k], dm), jnp.where(k < cs, ds + thick[k], ds)

    zero = jnp.zeros((span, LANES), jnp.float32)
    dm, ds = lax.fori_loop(0, layers, deepen, (zero, zero), unroll=4)
    em, es = east(dm, ds)
    em, es = jnp.minimum(dm, em), jnp.minimum(ds, es)
    nm, ns = jnp.minimum(dm, up(dm)), jnp.minimum(ds, up(ds))

    def take(buf, i):
        return buf[:, i].reshape(span, LANES)

    def gate(depth, flux):
        return jnp.where(depth > 0, TIMESTEP * flux, 0.0)

    own = slice(centre * r, centre * r + r)
    depth_e, depth_n = em[own], nm[own]
    xm, xs = gate(em, take(state, 1)), gate(es, take(state_side, 1))
    ym, ys = gate(nm, take(state, 2)), gate(ns, take(state_side, 2))

    def divergence(xm, xs, ym, ys):
        wm, ws = west(xm, xs)
        return (xm - wm) + (ym - down(ym)), (xs - ws) + (ys - down(ys))

    square = TIMESTEP * TIMESTEP
    aem, aes, anm, ans = square * em, square * es, square * nm, square * ns
    awm, aws = west(aem, aes)
    asm, ass = down(anm), down(ans)
    start_e, start_n = xm[own], ym[own]
    now = [take(state, 0), take(state_side, 0), *divergence(xm, xs, ym, ys)]
    fixed = [aem, aes, awm, aws, anm, ans, asm, ass, aem + awm + anm + asm, aes + aws + ans + ass]

    for c in lat_f + side_f:
        c.wait_recv()
    fe = jnp.concatenate([x for s in range(tiles) for x in (force_east[s], lanes(force_east[s], middle))], 0)
    fw = jnp.concatenate([x for s in range(tiles) for x in (lanes(force_west[s], middle), force_west[s])], 0)
    near = lane_of(fe) < middle
    fm_e, fm_n = take(force, 0), take(force, 1)
    fs_e = jnp.where(near, fe, fw)
    fs_n = jnp.where(near, lanes(fe, -quarter), lanes(fw, quarter))
    fixed += divergence(fm_e, fs_e, fm_n, fs_n)

    plan = [(NSUB, span, 0)]
    if tiles >= 3:
        plan = [(NSUB - 16, span, 0), (8, 3 * r, (centre - 1) * r), (8, 2 * r, centre * r - half)]
    size, low_row = plan[-1][1], plan[-1][2]
    weighted = (jnp.zeros((size, LANES), jnp.float32), jnp.zeros((size, LANES), jnp.float32))
    base, done = 0, 0
    for steps, rows, start in plan:
        cut = slice(start - base, start - base + rows)
        now = [x[cut] for x in now]
        fixed = [x[cut] for x in fixed]
        base = start
        mine = slice(low_row - base, low_row - base + size)

        def step(i, carry, mine=mine, fixed=fixed, done=done):
            hm, hs, zm, zs, um, us = carry
            aem, aes, awm, aws, anm, ans, asm, ass, acm, acs, dm, ds = fixed
            hm, hs = hm - zm, hs - zs
            (gm, gs), (wm, ws) = east(hm, hs), west(hm, hs)
            zm = zm + ((acm * hm + dm) - (aem * gm + awm * wm) - (anm * up(hm) + asm * down(hm)))
            zs = zs + ((acs * hs + ds) - (aes * gs + aws * ws) - (ans * up(hs) + ass * down(hs)))
            weight = (NSUB - done - i).astype(jnp.float32)
            return hm, hs, zm, zs, um + weight * hm[mine], us + weight * hs[mine]

        *now, um, us = lax.fori_loop(0, steps, step, (*now, *weighted))
        weighted = (um, us)
        done += steps
    um, us = weighted
    gm, _ = east(um, us)
    mine = slice(centre * r - base, centre * r - base + r)
    final = now[0][mine]
    ramp = NSUB * (NSUB + 1) / 2
    total_e = NSUB * start_e - square * depth_e * (gm - um)[mine] + ramp * sum_e
    total_n = NSUB * start_n - square * depth_n * (up(um) - um)[mine] + ramp * sum_n
    mean_e = total_e / (NSUB * TIMESTEP)
    mean_n = total_n / (NSUB * TIMESTEP)
    one = jnp.ones((r, LANES), jnp.float32)
    small[0] = final
    small[1] = mean_e
    small[2] = mean_n
    small[3] = (mean_e - column_e) / (depth_e + jnp.where(depth_e > 0, 0.0, one))
    small[4] = (mean_n - column_n) / (depth_n + jnp.where(depth_n > 0, 0.0, one))
    small[5] = face_e[:r].astype(jnp.float32)
    small[6] = face_n[:r].astype(jnp.float32)
    for c in started:
        c.wait_send()


def finish(after_e, after_n, small, oe, on, oh, ome, omn):
    oh[...] = small[0]
    ome[...] = small[1]
    omn[...] = small[2]
    face_e, face_n = small[5], small[6]
    shift_e, shift_n = small[3], small[4]

    def level(k, _):
        depth = k.astype(jnp.float32)
        oe[k] = jnp.where(depth < face_e, after_e[k] + shift_e, 0.0)
        on[k] = jnp.where(depth < face_n, after_n[k] + shift_n, 0.0)
        return 0

    lax.fori_loop(0, after_e.shape[0], level, 0, unroll=4)


def solution(mesh):
    nlon, nlat = mesh.shape["lon"], mesh.shape["lat"]

    def shards(ve, vn, cnt, height, te, tn, thick):
        layers, r, width = ve.shape
        reach = -(-NSUB // r)
        tiles = min(nlat, 2 * reach + 1)
        centre = tiles // 2
        ntiles = -(-2 * layers // PER_TILE)
        f32, i32 = jnp.float32, jnp.int32
        tile = (r, width)
        vm = pltpu.VMEM
        vspec = pl.BlockSpec(memory_space=pltpu.VMEM)
        copies = 2 + 8 + 2 + 4 + 6 + 2 + 9 * (tiles - 1)
        after_e, after_n, small = pl.pallas_call(
            functools.partial(kernel, nlon, nlat, tiles, centre),
            out_shape=(
                jax.ShapeDtypeStruct(ve.shape, f32),
                jax.ShapeDtypeStruct(ve.shape, f32),
                jax.ShapeDtypeStruct((7, *tile), f32),
            ),
            in_specs=[pl.BlockSpec(memory_space=pltpu.HBM)] * 7,
            out_specs=[vspec] * 3,
            scratch_shapes=[
                pltpu.SMEM((layers,), f32),
                vm(ve.shape, f32),
                vm(ve.shape, f32),
                vm(tile, i32),
                vm(tile, f32),
                vm(tile, f32),
                vm(tile, f32),
                pltpu.SemaphoreType.DMA((7,)),
                vm((layers, 8, width), f32),
                vm((layers, 8, width), f32),
                vm((ntiles, *tile), f32),
                vm((ntiles, *tile), f32),
                vm((ntiles, *tile), f32),
                vm((4, ntiles, 8, width), f32),
                vm((4, 8, width), i32),
                vm((ntiles, r + 8, width), f32),
                vm((tiles, 3, *tile), f32),
                vm((tiles, 3, *tile), f32),
                vm((3, *tile), f32),
                vm((3, *tile), f32),
                vm((tiles, *tile), i32),
                vm((tiles, *tile), i32),
                vm(tile, i32),
                vm(tile, i32),
                vm((tiles, 2, *tile), f32),
                vm((2, 8, width), f32),
                vm((tiles, 8, width), f32),
                vm((tiles, 8, width), f32),
                pltpu.SemaphoreType.DMA((copies,)),
                pltpu.SemaphoreType.DMA((copies,)),
            ],
            compiler_params=pltpu.CompilerParams(
                collective_id=0, has_side_effects=True, vmem_limit_bytes=16 << 20),
        )(*[pltpu.with_memory_space_constraint(x, pltpu.HBM) for x in (thick, ve, vn, cnt, height, te, tn)])
        out = jax.ShapeDtypeStruct(tile, f32)
        levels = jax.ShapeDtypeStruct(ve.shape, f32)
        return pl.pallas_call(
            finish,
            out_shape=(levels, levels, out, out, out),
            in_specs=[vspec] * 3,
            out_specs=[vspec] * 5,
            compiler_params=pltpu.CompilerParams(vmem_limit_bytes=16 << 20),
        )(after_e, after_n, small)

    level = P(None, "lat", "lon")
    flat = P("lat", "lon")
    return jax.shard_map(
        shards,
        mesh=mesh,
        in_specs=(level, level, flat, flat, flat, flat, P()),
        out_specs=(level, level, flat, flat, flat),
        check_vma=False,
    )
```

```python
import functools

import jax
import jax.numpy as jnp
from jax import lax
from jax.experimental import pallas as pl
from jax.experimental.pallas import tpu as pltpu
from jax.sharding import PartitionSpec as P

NSUB = 30
VISCOSITY = 0.01
TIMESTEP = 0.35
LANES = 128
GROUP = 4
PER_TILE = LANES // GROUP
UNROLL = 8
MESH = pl.DeviceIdType.MESH


def lane_of(x):
    return lax.broadcasted_iota(jnp.int32, x.shape, 1)


def sub_of(x):
    return lax.broadcasted_iota(jnp.int32, x.shape, 0)


def lanes(x, shift):
    return pltpu.roll(x, shift % LANES, 1)


def up(x):
    return pltpu.roll(x, x.shape[0] - 1, 0)


def down(x):
    return pltpu.roll(x, 1, 0)


def east(main, side):
    a, b = lanes(main, -1), lanes(side, -1)
    last = lane_of(main) == LANES - 1
    return jnp.where(last, b, a), jnp.where(last, a, b)


def west(main, side):
    a, b = lanes(main, 1), lanes(side, 1)
    first = lane_of(main) == 0
    return jnp.where(first, b, a), jnp.where(first, a, b)


def segments(layers):
    found, q = [], 0
    for field in range(2):
        k = 0
        while k < layers:
            n = min(layers - k, PER_TILE - q % PER_TILE)
            found.append((field, k, n, q // PER_TILE, q % PER_TILE))
            k, q = k + n, q + n
    return found


def kernel(
    nlon, nlat, tiles, centre,
    thick_hbm, ve_hbm, vn_hbm, cnt_hbm, height_hbm, te_hbm, tn_hbm,
    oe, on, small,
    thick, ve, vn, cnt, height, te, tn, loads,
    rows_e, rows_n, packed, from_east, from_west, corner, corner_count, inject,
    state, state_side, state_east, state_west,
    count, count_side, count_east, count_west,
    force, force_out, force_east, force_west,
    send, recv,
):
    layers, r, _ = ve.shape
    lon, lat = lax.axis_index("lon"), lax.axis_index("lat")
    offsets = [o for o in range(centre - tiles + 1, centre + 1) if o != 0]

    def device(dx, dy):
        return {"lon": lax.rem(lon + nlon + dx, nlon), "lat": lax.rem(lat + nlat + dy, nlat)}

    partners = [(1, 0), (-1, 0)] + [(0, o) for o in offsets]
    partners += [(dx, o) for dx in (1, -1) for o in offsets]
    barrier = pltpu.get_barrier_semaphore()
    for dx, dy in partners:
        pl.semaphore_signal(barrier, inc=1, device_id=device(dx, dy), device_id_type=MESH)

    fetched = []
    for i, (far, near) in enumerate((
        (ve_hbm, ve), (vn_hbm, vn), (cnt_hbm, cnt), (height_hbm, height), (te_hbm, te), (tn_hbm, tn),
        (thick_hbm, thick),
    )):
        fetched.append(pltpu.make_async_copy(far, near, loads.at[i]))
        fetched[-1].start()

    used = [0]
    started = []

    def push(src, dst, dx, dy):
        i = used[0]
        used[0] += 1
        c = pltpu.make_async_remote_copy(
            src_ref=src, dst_ref=dst, send_sem=send.at[i], recv_sem=recv.at[i],
            device_id=device(dx, dy), device_id_type=MESH)
        c.start()
        started.append(c)
        return c

    for c in fetched:
        c.wait()

    ntiles = packed.shape[0]
    for t in range(ntiles):
        acc = jnp.zeros((r, LANES), jnp.float32)
        for field, k0, n, tile, m0 in segments(layers):
            if tile != t:
                continue
            v = (ve, vn)[field]

            def put(i, acc, v=v, k0=k0, m0=m0):
                m = m0 + i
                x = pltpu.roll(v[k0 + i], GROUP * m + 2 - LANES * ((GROUP * m + 2) // LANES), 1)
                return jnp.where(lane_of(x) // GROUP == m, x, acc)

            acc = lax.fori_loop(0, n, put, acc, unroll=4)
        packed[t] = acc
    pl.semaphore_wait(barrier, len(partners))

    lon_c = [push(cnt, count_west, 1, 0), push(cnt, count_east, -1, 0)]
    diag_c, diag_v, lat_v = [], [], []
    diag = [(-1, -1, 0), (-1, 1, 1), (1, -1, 2), (1, 1, 3)]
    half = r // 2
    for dx, dy, slot in diag:
        part = pl.ds(0, 8) if dy < 0 else pl.ds(r - 8, 8)
        diag_c.append(push(cnt.at[part], corner_count.at[slot], dx, dy))
    lat_c = [push(cnt, count.at[centre - o], 0, o) for o in offsets]
    for dx, dy, slot in diag:
        part = pl.ds(0, 8) if dy < 0 else pl.ds(r - 8, 8)
        diag_v.append(push(packed.at[:, part], corner.at[slot], dx, dy))
    lon_v = [push(packed, from_west, 1, 0), push(packed, from_east, -1, 0)]
    for v, buf in ((ve, rows_e), (vn, rows_n)):
        lat_v.append(push(v.at[:, pl.ds(0, 2)], buf.at[:, pl.ds(0, 2)], 0, -1))
        lat_v.append(push(v.at[:, pl.ds(r - 2, 2)], buf.at[:, pl.ds(6, 2)], 0, 1))
    fields = (height, te, tn)
    lon_s = []
    for i, f in enumerate(fields):
        lon_s.append(push(f, state_west.at[i], 1, 0))
        lon_s.append(push(f, state_east.at[i], -1, 0))
    lat_s = [push(f, state.at[centre - o, i], 0, o) for i, f in enumerate(fields) for o in offsets]
    count[centre] = cnt[...]
    for i, f in enumerate(fields):
        state[centre, i] = f[...]

    right = lax.broadcasted_iota(jnp.int32, (r, LANES), 1) < LANES // 2
    for c in lon_c + diag_c + lat_c:
        c.wait_recv()

    low = lax.broadcasted_iota(jnp.int32, (8, LANES), 0) < 4

    def ring(x, north, south):
        return jnp.concatenate([x, jnp.where(low, north, south)], 0)

    c24 = ring(cnt[...], count[(centre + 1) % tiles, 0:8], count[(centre - 1) % tiles, r - 8:r])
    ce = ring(count_east[...], corner_count[0], corner_count[1])
    cw = ring(count_west[...], corner_count[2], corner_count[3])
    lane = lane_of(c24)
    face_e = jnp.minimum(c24, jnp.where(lane == LANES - 1, lanes(ce, -1), lanes(c24, -1)))
    face_n = jnp.minimum(c24, up(c24))

    def spread(x):
        x = jnp.where(lane < 2, x, 0)
        step = GROUP
        while step < LANES:
            x = x + lanes(x, step)
            step *= 2
        return x

    inner = spread(jnp.where(lane == 0, ce, lanes(cw, 2)))
    outer = spread(jnp.where(lane == 0, lanes(ce, -1), lanes(c24, 1)))
    edge_e = jnp.minimum(inner, outer)[:r]
    edge_n = jnp.minimum(inner, up(inner))[:r]
    slot16 = lax.broadcasted_iota(jnp.int32, (r, LANES), 1)
    place = slot16 % GROUP
    for c in lon_v + diag_v:
        c.wait_recv()
    for t in range(ntiles):
        fe = ring(from_east[t], corner[0, t], corner[1, t])
        fw = ring(from_west[t], corner[2, t], corner[3, t])
        g = jnp.where(lane % GROUP == 0, lanes(fe, -2), fw)
        across = jnp.where(place == 0, lanes(fe[:r], -3), lanes(fw[:r], 1)) + lanes(packed[t], -1)
        q = t * PER_TILE + slot16 // GROUP
        k = jnp.where(q < layers, q, q - layers)
        wet = k < jnp.where(q < layers, edge_e, edge_n)
        e = jnp.where(wet, across + up(g)[:r] + down(g)[:r] - 4.0 * g[:r], 0.0)
        inject[t, 0:r] = jnp.where(place < 2, g[:r], lanes(e, 2))
        inject[t, r:r + 8] = g[r:]

    first, last = lane == 0, lane == LANES - 1
    first16, last16 = first[:r], last[:r]
    for c in lat_v:
        c.wait_recv()
    sums, side_c, side_s = [], [], []
    for field, (v, buf, face, out) in enumerate(((ve, rows_e, face_e, oe), (vn, rows_n, face_n, on))):

        def level(k, carry, field=field, v=v, buf=buf, face=face, out=out):
            total, column = carry
            q = field * layers + k
            t = q // PER_TILE
            m = q - t * PER_TILE
            own = v[k]
            x = jnp.concatenate([own, buf[k]], 0)
            j = inject[t]
            turn = LANES - 1 - GROUP * m
            turn = jnp.where(turn < 0, turn + LANES, turn)
            rim = pltpu.roll(j, turn, 1)
            rim2 = pltpu.roll(j[:r], jnp.where(turn < 2, turn + LANES - 2, turn - 2), 1)
            wet = k < face
            l1 = (jnp.where(last, rim, lanes(x, -1)) + jnp.where(first, rim, lanes(x, 1))
                  + up(x) + down(x) - 4.0 * x)
            l1 = jnp.where(wet, l1, 0.0)
            mid = l1[:r]
            l2 = (jnp.where(last16, rim2, lanes(mid, -1)) + jnp.where(first16, rim2, lanes(mid, 1))
                  + up(l1)[:r] + down(l1)[:r] - 4.0 * mid)
            tend = jnp.where(wet[:r], -VISCOSITY * l2, 0.0)
            after = own + tend
            out[k] = after
            return total + thick[k] * tend, column + thick[k] * after

        zero = jnp.zeros((r, LANES), jnp.float32)
        sums.append(lax.fori_loop(0, layers, level, (zero, zero), unroll=UNROLL))
        if field == 0:
            for c in lon_s:
                c.wait_recv()
            count_side[centre] = jnp.where(right, count_east[...], count_west[...])
            for i in range(3):
                state_side[centre, i] = jnp.where(right, state_east[i], state_west[i])
            side_c = [push(count_side.at[centre], count_side.at[centre - o], 0, o) for o in offsets]
            side_s = [push(state_side.at[centre], state_side.at[centre - o], 0, o) for o in offsets]
    (sum_e, column_e), (sum_n, column_n) = sums
    sum_e, sum_n = sum_e * (TIMESTEP / NSUB), sum_n * (TIMESTEP / NSUB)
    force[centre, 0] = sum_e
    force[centre, 1] = sum_n
    quarter, middle = LANES // 4, LANES // 2
    out = jnp.where(slot16 >= LANES - quarter, sum_e, lanes(sum_n, -quarter))
    force_out[0] = jnp.where(right[:8], lanes(out[:8], middle), out[8:])
    out = jnp.where(slot16 < quarter, sum_e, lanes(sum_n, quarter))
    force_out[1] = jnp.where(right[:8], out[:8], lanes(out[8:], middle))
    side_f = []
    for o in [0] + offsets:
        side_f.append(push(force_out.at[0], force_west.at[centre - o], 1, o))
        side_f.append(push(force_out.at[1], force_east.at[centre - o], -1, o))
    lat_f = [push(force.at[centre], force.at[centre - o], 0, o) for o in offsets]

    for c in side_c + side_s + lat_s:
        c.wait_recv()
    span = tiles * r
    cm, cs = count[...].reshape(span, LANES), count_side[...].reshape(span, LANES)

    def deepen(k, carry):
        dm, ds = carry
        return jnp.where(k < cm, dm + thick[k], dm), jnp.where(k < cs, ds + thick[k], ds)

    zero = jnp.zeros((span, LANES), jnp.float32)
    dm, ds = lax.fori_loop(0, layers, deepen, (zero, zero), unroll=4)
    em, es = east(dm, ds)
    em, es = jnp.minimum(dm, em), jnp.minimum(ds, es)
    nm, ns = jnp.minimum(dm, up(dm)), jnp.minimum(ds, up(ds))

    def take(buf, i):
        return buf[:, i].reshape(span, LANES)

    def gate(depth, flux):
        return jnp.where(depth > 0, TIMESTEP * flux, 0.0)

    own = slice(centre * r, centre * r + r)
    depth_e, depth_n = em[own], nm[own]
    xm, xs = gate(em, take(state, 1)), gate(es, take(state_side, 1))
    ym, ys = gate(nm, take(state, 2)), gate(ns, take(state_side, 2))

    def divergence(xm, xs, ym, ys):
        wm, ws = west(xm, xs)
        return (xm - wm) + (ym - down(ym)), (xs - ws) + (ys - down(ys))

    square = TIMESTEP * TIMESTEP
    aem, aes, anm, ans = square * em, square * es, square * nm, square * ns
    awm, aws = west(aem, aes)
    asm, ass = down(anm), down(ans)
    start_e, start_n = xm[own], ym[own]
    now = [take(state, 0), take(state_side, 0), *divergence(xm, xs, ym, ys)]
    fixed = [aem, aes, awm, aws, anm, ans, asm, ass, aem + awm + anm + asm, aes + aws + ans + ass]

    for c in lat_f + side_f:
        c.wait_recv()
    fe = jnp.concatenate([x for s in range(tiles) for x in (force_east[s], lanes(force_east[s], middle))], 0)
    fw = jnp.concatenate([x for s in range(tiles) for x in (lanes(force_west[s], middle), force_west[s])], 0)
    near = lane_of(fe) < middle
    fm_e, fm_n = take(force, 0), take(force, 1)
    fs_e = jnp.where(near, fe, fw)
    fs_n = jnp.where(near, lanes(fe, -quarter), lanes(fw, quarter))
    fixed += divergence(fm_e, fs_e, fm_n, fs_n)

    plan = [(NSUB, span, 0)]
    if tiles >= 3:
        plan = [(NSUB - 16, span, 0), (8, 3 * r, (centre - 1) * r), (8, 2 * r, centre * r - half)]
    size, low_row = plan[-1][1], plan[-1][2]
    weighted = (jnp.zeros((size, LANES), jnp.float32), jnp.zeros((size, LANES), jnp.float32))
    base, done = 0, 0
    for steps, rows, start in plan:
        cut = slice(start - base, start - base + rows)
        now = [x[cut] for x in now]
        fixed = [x[cut] for x in fixed]
        base = start
        mine = slice(low_row - base, low_row - base + size)

        def step(i, carry, mine=mine, fixed=fixed, done=done):
            hm, hs, zm, zs, um, us = carry
            aem, aes, awm, aws, anm, ans, asm, ass, acm, acs, dm, ds = fixed
            hm, hs = hm - zm, hs - zs
            (gm, gs), (wm, ws) = east(hm, hs), west(hm, hs)
            zm = zm + ((acm * hm + dm) - (aem * gm + awm * wm) - (anm * up(hm) + asm * down(hm)))
            zs = zs + ((acs * hs + ds) - (aes * gs + aws * ws) - (ans * up(hs) + ass * down(hs)))
            weight = (NSUB - done - i).astype(jnp.float32)
            return hm, hs, zm, zs, um + weight * hm[mine], us + weight * hs[mine]

        *now, um, us = lax.fori_loop(0, steps, step, (*now, *weighted))
        weighted = (um, us)
        done += steps
    um, us = weighted
    gm, _ = east(um, us)
    mine = slice(centre * r - base, centre * r - base + r)
    final = now[0][mine]
    ramp = NSUB * (NSUB + 1) / 2
    total_e = NSUB * start_e - square * depth_e * (gm - um)[mine] + ramp * sum_e
    total_n = NSUB * start_n - square * depth_n * (up(um) - um)[mine] + ramp * sum_n
    mean_e = total_e / (NSUB * TIMESTEP)
    mean_n = total_n / (NSUB * TIMESTEP)
    one = jnp.ones((r, LANES), jnp.float32)
    small[0] = final
    small[1] = mean_e
    small[2] = mean_n
    small[3] = (mean_e - column_e) / (depth_e + jnp.where(depth_e > 0, 0.0, one))
    small[4] = (mean_n - column_n) / (depth_n + jnp.where(depth_n > 0, 0.0, one))
    small[5] = face_e[:r].astype(jnp.float32)
    small[6] = face_n[:r].astype(jnp.float32)
    for c in started:
        c.wait_send()


def finish(after_e, after_n, small, oe, on, oh, ome, omn):
    oh[...] = small[0]
    ome[...] = small[1]
    omn[...] = small[2]
    face_e, face_n = small[5], small[6]
    shift_e, shift_n = small[3], small[4]

    def level(k, _):
        depth = k.astype(jnp.float32)
        oe[k] = jnp.where(depth < face_e, after_e[k] + shift_e, 0.0)
        on[k] = jnp.where(depth < face_n, after_n[k] + shift_n, 0.0)
        return 0

    lax.fori_loop(0, after_e.shape[0], level, 0, unroll=4)


def solution(mesh):
    nlon, nlat = mesh.shape["lon"], mesh.shape["lat"]

    def shards(ve, vn, cnt, height, te, tn, thick):
        layers, r, width = ve.shape
        reach = -(-NSUB // r)
        tiles = min(nlat, 2 * reach + 1)
        centre = tiles // 2
        ntiles = -(-2 * layers // PER_TILE)
        f32, i32 = jnp.float32, jnp.int32
        tile = (r, width)
        vm = pltpu.VMEM
        vspec = pl.BlockSpec(memory_space=pltpu.VMEM)
        copies = 2 + 8 + 2 + 4 + 6 + 2 + 9 * (tiles - 1)
        after_e, after_n, small = pl.pallas_call(
            functools.partial(kernel, nlon, nlat, tiles, centre),
            out_shape=(
                jax.ShapeDtypeStruct(ve.shape, f32),
                jax.ShapeDtypeStruct(ve.shape, f32),
                jax.ShapeDtypeStruct((7, *tile), f32),
            ),
            in_specs=[pl.BlockSpec(memory_space=pltpu.HBM)] * 7,
            out_specs=[vspec] * 3,
            scratch_shapes=[
                pltpu.SMEM((layers,), f32),
                vm(ve.shape, f32),
                vm(ve.shape, f32),
                vm(tile, i32),
                vm(tile, f32),
                vm(tile, f32),
                vm(tile, f32),
                pltpu.SemaphoreType.DMA((7,)),
                vm((layers, 8, width), f32),
                vm((layers, 8, width), f32),
                vm((ntiles, *tile), f32),
                vm((ntiles, *tile), f32),
                vm((ntiles, *tile), f32),
                vm((4, ntiles, 8, width), f32),
                vm((4, 8, width), i32),
                vm((ntiles, r + 8, width), f32),
                vm((tiles, 3, *tile), f32),
                vm((tiles, 3, *tile), f32),
                vm((3, *tile), f32),
                vm((3, *tile), f32),
                vm((tiles, *tile), i32),
                vm((tiles, *tile), i32),
                vm(tile, i32),
                vm(tile, i32),
                vm((tiles, 2, *tile), f32),
                vm((2, 8, width), f32),
                vm((tiles, 8, width), f32),
                vm((tiles, 8, width), f32),
                pltpu.SemaphoreType.DMA((copies,)),
                pltpu.SemaphoreType.DMA((copies,)),
            ],
            compiler_params=pltpu.CompilerParams(
                collective_id=0, has_side_effects=True, vmem_limit_bytes=16 << 20),
        )(*[pltpu.with_memory_space_constraint(x, pltpu.HBM) for x in (thick, ve, vn, cnt, height, te, tn)])
        out = jax.ShapeDtypeStruct(tile, f32)
        levels = jax.ShapeDtypeStruct(ve.shape, f32)
        return pl.pallas_call(
            finish,
            out_shape=(levels, levels, out, out, out),
            in_specs=[vspec] * 3,
            out_specs=[vspec] * 5,
            compiler_params=pltpu.CompilerParams(vmem_limit_bytes=16 << 20),
        )(after_e, after_n, small)

    level = P(None, "lat", "lon")
    flat = P("lat", "lon")
    return jax.shard_map(
        shards,
        mesh=mesh,
        in_specs=(level, level, flat, flat, flat, flat, P()),
        out_specs=(level, level, flat, flat, flat),
        check_vma=False,
    )
```
